32 devices in a mesh: row: 4 (over y, core), col: 8 (over z, x).
Axes of the slice: x: 2, y: 2, z: 4, core: 2. Of those that a mesh axis runs over, the one named last changes fastest.
Arguments:
- factor: float32 [24, 262144], P(None, ('row', 'col')), may hold values from -1.2 to 1.2
- prior: float32 [24, 262144], P(None, ('row', 'col')), may hold values from -1.2 to 1.2
- tile_src: int32 [32, 384], P(('row', 'col')), may hold values from 0 to 63
- tile_dst: int32 [32, 384], P(('row', 'col')), may hold values from 0 to 63
- tile_count: int32 [32], P(('row', 'col')), may hold values from 96 to 384, as said below
- tile_vals: bfloat16 [12288, 128, 128], P(('row', 'col'))
- sep_idx: int32 [32, 4, 256], P(('row', 'col')), may hold values from 0 to 8191, as said below
- sep_count: int32 [32, 4], P(('row', 'col')), may hold values from 64 to 256, as said below
- couple: bfloat16 [32, 4, 256, 256], P(('row', 'col')), may hold values from -0.1875 to 0.1875
- masks: int32 [4], replicated, may hold values from 1 to 31, as said below
Outputs:
- new_factor: float32 [24, 262144], P(None, ('row', 'col'))
- momentum: float32 [], replicated
- energy: float32 [], replicated
The draws below stay inside these ranges and needn't reach their ends.
Inputs may be any that keep to these rules, and one draw needn't show every extreme that they name: `tile_count`: some partition has all 384 slots live; slots at or beyond a partition's count are padding. `sep_idx`: distinct within one partition and round. `sep_count`: in every round some partition has all 256 slots live. masks[0] is 31, masks[1] is 16 and the last round's mask is 1.
All inputs are finite; a program needn't handle non-finite values.
Results may differ from the reference program's by a relative error of at most 0.0031.
Values may be sent and summed in bfloat16 or wider, within the bound.
A program may use at most 128 MiB of HBM per device.

```python
import jax
import jax.numpy as jnp
from jax import lax

R = 24
TILE = 128
ROUNDS = 4
ITERS = 2
NODE_DEV = 8192
TILES_DEV = 384
SEP = 256
PARTS_SIZE = 32
NB = 64
NODES = 262144


def draw_tile_vals(key, part):
    position = jnp.arange(PARTS_SIZE, dtype=jnp.float32) / max(PARTS_SIZE - 1, 1)
    spread = 0.6 * (1.0 + 2.0 * position) / jnp.sqrt(5.0 * TILE)
    scaling = jnp.repeat(spread, TILES_DEV)[:, None, None]
    base = jax.random.normal(key, (PARTS_SIZE * TILES_DEV, TILE, TILE), jnp.float32)
    return (base * scaling).astype(jnp.bfloat16)


def draw_sep_idx(key, part):
    subkeys = jax.random.split(jax.random.fold_in(key, 11), PARTS_SIZE * ROUNDS)

    def pick_nodes(subkey):
        return jax.random.permutation(subkey, NODE_DEV)[:SEP]
    chosen = jax.vmap(pick_nodes)(subkeys)
    return chosen.reshape(PARTS_SIZE, ROUNDS, SEP).astype(jnp.int32)


def draw_sep_count(key, part):
    first_key = jax.random.fold_in(key, 21)
    second_key = jax.random.fold_in(key, 22)
    base = jax.random.randint(first_key, (PARTS_SIZE, ROUNDS), SEP // 4, SEP + 1)
    fullest = jax.random.randint(second_key, (ROUNDS,), 0, PARTS_SIZE)
    hit = jnp.arange(PARTS_SIZE, dtype=jnp.int32)[:, None] == fullest[None, :]
    return jnp.where(hit, SEP, base).astype(jnp.int32)


def draw_tile_count(key, part):
    first_key = jax.random.fold_in(key, 31)
    second_key = jax.random.fold_in(key, 32)
    shifts = jax.random.randint(first_key, (PARTS_SIZE,), 0, 3)
    base = jnp.right_shift(jnp.full((PARTS_SIZE,), TILES_DEV, jnp.int32), shifts)
    fullest = jax.random.randint(second_key, (), 0, PARTS_SIZE)
    return jnp.where(jnp.arange(PARTS_SIZE, dtype=jnp.int32) == fullest, TILES_DEV, base).astype(jnp.int32)


def draw_masks(key, part):
    middle = jax.random.randint(jax.random.fold_in(key, 41), (ROUNDS,), 1, PARTS_SIZE)
    middle = middle.at[0].set(PARTS_SIZE - 1)
    middle = middle.at[1].set(PARTS_SIZE // 2)
    middle = middle.at[ROUNDS - 1].set(1)
    return middle.astype(jnp.int32)


def place_ends(drawn, stream_key, low, largest):
    longest = drawn.shape.index(max(drawn.shape))
    spots = []
    for shift in (0, 1):
        where = [jax.random.randint(jax.random.fold_in(stream_key, axis), (), 0, length) for axis, length in enumerate(drawn.shape)]
        where[longest] = (where[longest] + shift) % drawn.shape[longest]
        spots.append(tuple(where))
    return drawn.at[spots[0]].set(low).at[spots[1]].set(largest)


def steps_of(stream_key, dims, shards, smallest, top_value):
    def one(dim, shards_of):
        heights = jax.random.uniform(jax.random.fold_in(jax.random.fold_in(stream_key, 6), dim), (shards_of,), jnp.float32, smallest / len(shards), top_value / len(shards))
        return jnp.repeat(jnp.exp(heights), dims[dim] // shards_of).reshape((-1,) + (1,) * (len(dims) - dim - 1))

    loudness = one(*shards[0])
    for cut in shards[1:]:
        loudness = loudness * one(*cut)
    return loudness


def scatter_about(own_key, dims, width, bound, cuts=(), kind=jnp.bfloat16):
    values = width * jax.random.normal(own_key, dims, jnp.float32)
    if cuts:
        values = values * steps_of(own_key, dims, cuts, -0.22, 0.18)
    return jnp.clip(values, -bound, bound).astype(kind)


def setup_inputs(seed: int = 0) -> dict:
    arg_keys = jax.random.split(jax.random.key(seed), 11)
    factor = scatter_about(arg_keys[0], (R, NODES), 0.2, 1.2, ((1, 32),), jnp.float32)
    prior = scatter_about(arg_keys[1], (R, NODES), 0.2, 1.2, ((1, 32),), jnp.float32)
    tile_src = place_ends(jax.random.randint(arg_keys[2], (PARTS_SIZE, TILES_DEV), 0, NB), jax.random.fold_in(arg_keys[2], 1), 0, NB - 1).astype(jnp.int32)
    tile_dst = place_ends(jax.random.randint(arg_keys[3], (PARTS_SIZE, TILES_DEV), 0, NB), jax.random.fold_in(arg_keys[3], 1), 0, NB - 1).astype(jnp.int32)
    tile_count = draw_tile_count(jax.random.fold_in(arg_keys[10], 71), 0)
    tile_vals = draw_tile_vals(jax.random.fold_in(arg_keys[10], 71), 0)
    sep_idx = draw_sep_idx(jax.random.fold_in(arg_keys[10], 71), 0)
    sep_count = draw_sep_count(jax.random.fold_in(arg_keys[10], 71), 0)
    couple = scatter_about(arg_keys[8], (PARTS_SIZE, ROUNDS, SEP, SEP), (4 * SEP) ** -0.5, 0.1875, ((0, 32),))
    masks = draw_masks(jax.random.fold_in(arg_keys[10], 71), 0)
    return {"factor": factor, "prior": prior, "tile_src": tile_src, "tile_dst": tile_dst, "tile_count": tile_count, "tile_vals": tile_vals, "sep_idx": sep_idx, "sep_count": sep_count, "couple": couple, "masks": masks}


MOMENTUM_CAP = 0.9

def tile_apply(inputs):
    grouped, sources, targets, live_count, values = inputs
    picked = jnp.take(grouped, sources, axis=1).astype(jnp.float32)
    products = jnp.einsum('rtk,tkc->rtc', picked, values.astype(jnp.float32), precision=lax.Precision.HIGHEST)
    live_tiles = (jnp.arange(sources.shape[0]) < live_count).astype(jnp.float32)
    dst_table = (targets[None, :] == jnp.arange(grouped.shape[1], dtype=jnp.int32)[:, None]).astype(jnp.float32) * live_tiles[None, :]
    return jnp.einsum('bt,rtc->rbc', dst_table, products, precision=lax.Precision.HIGHEST)

def add_columns(target, columns, extra):
    return target.at[:, columns].add(extra)

def operate(packed, tile_src, tile_dst, tile_count, tile_vals, sep_idx, sep_count, couple, masks):
    grouped_all = packed.reshape(R, PARTS_SIZE, NB, TILE).transpose(1, 0, 2, 3)
    values_all = tile_vals.reshape(PARTS_SIZE, TILES_DEV, TILE, TILE)
    applied_dev = lax.map(tile_apply, (grouped_all, tile_src, tile_dst, tile_count, values_all))
    applied_dev = applied_dev.reshape(PARTS_SIZE, R, NODE_DEV)
    packed_dev = packed.reshape(R, PARTS_SIZE, NODE_DEV).transpose(1, 0, 2)
    for rnd in range(ROUNDS):
        columns = sep_idx[:, rnd, :]
        keep = jnp.arange(SEP, dtype=jnp.int32)[None, :] < sep_count[:, rnd][:, None]
        picked = jnp.take_along_axis(packed_dev, columns[:, None, :], axis=2)
        sent = jnp.where(keep[:, None, :], picked, jnp.zeros_like(picked))
        partner = jnp.arange(PARTS_SIZE, dtype=jnp.int32) ^ masks[rnd]
        received = sent[partner].astype(jnp.float32)
        extra = jnp.einsum('prs,pst->prt', received, couple[:, rnd].astype(jnp.float32), precision=lax.Precision.HIGHEST)
        extra = jnp.where(keep[:, None, :], extra, jnp.zeros_like(extra))
        applied_dev = jax.vmap(add_columns)(applied_dev, columns, extra)
    return applied_dev.transpose(1, 0, 2).reshape(R, NODES)

def reference(factor, prior, tile_src, tile_dst, tile_count, tile_vals, sep_idx, sep_count, couple, masks):
    current = factor
    previous = prior
    beta = jnp.float32(0.5 * MOMENTUM_CAP)
    energy = jnp.float32(0.0)
    for iterate in range(ITERS):
        blend = current + beta * (current - previous)
        packed = blend.astype(jnp.bfloat16)
        applied = operate(packed, tile_src, tile_dst, tile_count, tile_vals, sep_idx, sep_count, couple, masks)
        moved = blend + applied
        length = jnp.sqrt(lax.optimization_barrier(jnp.sum(moved * moved, axis=0, keepdims=True)))
        updated = moved / jnp.maximum(length, 1.0)
        change = jnp.sum(applied * (updated - current))
        energy = jnp.sum(applied * updated) / NODES
        beta = MOMENTUM_CAP * 0.5 * (1.0 + jnp.tanh(change / NODES))
        previous = current
        current = updated
    return (current, beta, energy)
```

```python
import functools

import jax
import jax.numpy as jnp
from jax import lax
from jax.experimental import pallas as pl
from jax.experimental.pallas import tpu as pltpu
from jax.sharding import PartitionSpec as P

TILE = 128
ITERS = 2
MOMENTUM_CAP = 0.9
MESH = pl.DeviceIdType.MESH
LIMIT = 60 * 1024 * 1024


def flip(x, j):
    bit = 1
    while bit <= j:
        if j & bit:
            x = x + bit * (1 - 2 * ((x // bit) % 2))
        bit *= 2
    return x


def step_kernel(mode, rows, cols, nodes_all, *refs):
    first, last = mode == "first", mode == "last"
    parts = rows * cols
    refs = list(refs)
    take = lambda n: [refs.pop(0) for _ in range(n)]
    if not last:
        idx_ref, cnt_ref, masks_ref = take(3)
    if first:
        cur_ref, prior_ref = take(2)
    else:
        cur_ref, blend_ref, app_ref = take(3)
    if not first:
        new_ref = take(1)[0]
    if not last:
        nblend_ref, packed_ref, recv_ref = take(3)
    else:
        beta_ref, energy_ref = take(2)
    if not first:
        stat, srow, scol = take(3)
        st_send, st_rrow, st_rcol = take(3)
    if not last:
        xt, gt, sbuf, direct, brow, bcol, picked = take(7)
        d_send, d_recv, c_send, c_recv, r_send, r_recv = take(6)

    comps = cur_ref.shape[0]
    blocks = cur_ref.shape[1] // TILE
    r = lax.axis_index("row")
    c = lax.axis_index("col")

    barrier = pltpu.get_barrier_semaphore()
    peers = [(flip(r, j), c) for j in range(1, rows)] + [(r, flip(c, j)) for j in range(1, cols)]
    if not last:
        peers.append((flip(r, rows - 1), flip(c, cols - 1)))
    for peer in peers:
        pl.semaphore_signal(barrier, inc=1, device_id=peer, device_id_type=MESH)

    def lanes(b):
        return pl.ds(pl.multiple_of(b * TILE, TILE), TILE)

    if first:
        pl.semaphore_wait(barrier, len(peers))
        beta = 0.5 * MOMENTUM_CAP
    else:
        def norm_block(b, carry):
            change, total = carry
            applied = app_ref[:, lanes(b)]
            moved = blend_ref[:, lanes(b)] + applied
            length = jnp.sqrt(jnp.sum(moved * moved, axis=0, keepdims=True))
            updated = moved / jnp.maximum(length, 1.0)
            new_ref[:, lanes(b)] = updated
            return (change + applied * (updated - cur_ref[:, lanes(b)]), total + applied * updated)

        zero = jnp.zeros((comps, TILE), jnp.float32)
        change, total = lax.fori_loop(0, blocks, norm_block, (zero, zero), unroll=4)
        stat[...] = jnp.zeros_like(stat)
        stat[0, 0:1, :] = jnp.sum(change, axis=0, keepdims=True)
        stat[0, 1:2, :] = jnp.sum(total, axis=0, keepdims=True)
        pl.semaphore_wait(barrier, len(peers))
        copies = []
        for j in range(1, rows):
            copies.append(pltpu.make_async_remote_copy(
                src_ref=stat.at[0], dst_ref=srow.at[r], send_sem=st_send.at[j],
                recv_sem=st_rrow.at[r], device_id=(flip(r, j), c), device_id_type=MESH))
        for copy in copies:
            copy.start()
        for j in range(1, rows):
            q = flip(r, j)
            pltpu.make_async_remote_copy(
                src_ref=stat.at[0], dst_ref=srow.at[q], send_sem=st_send.at[j],
                recv_sem=st_rrow.at[q], device_id=(q, c), device_id_type=MESH).wait_recv()
        mine = stat[0]
        both = jnp.where(r == 0, mine, srow[0])
        for q in range(1, rows):
            both = both + jnp.where(r == q, mine, srow[q])
        stat[1] = both
        more = []
        for j in range(1, cols):
            more.append(pltpu.make_async_remote_copy(
                src_ref=stat.at[1], dst_ref=scol.at[c], send_sem=st_send.at[rows + j],
                recv_sem=st_rcol.at[c], device_id=(r, flip(c, j)), device_id_type=MESH))
        for copy in more:
            copy.start()
        for j in range(1, cols):
            q = flip(c, j)
            pltpu.make_async_remote_copy(
                src_ref=stat.at[1], dst_ref=scol.at[q], send_sem=st_send.at[rows + j],
                recv_sem=st_rcol.at[q], device_id=(r, q), device_id_type=MESH).wait_recv()
        both = stat[1]
        every = jnp.where(c == 0, both, scol[0])
        for q in range(1, cols):
            every = every + jnp.where(c == q, both, scol[q])
        sums = jnp.sum(every, axis=1, keepdims=True) / nodes_all
        beta = MOMENTUM_CAP * 0.5 * (1.0 + jnp.tanh(sums[0:1]))
        if last:
            beta_ref[...] = jnp.broadcast_to(beta, beta_ref.shape)
            energy_ref[...] = jnp.broadcast_to(sums[1:2], energy_ref.shape)
        for copy in copies + more:
            copy.wait_send()

    if last:
        return

    rounds, slots = idx_ref.shape

    def blend_block(b, carry):
        if first:
            now, before = cur_ref[:, lanes(b)], prior_ref[:, lanes(b)]
        else:
            now, before = new_ref[:, lanes(b)], cur_ref[:, lanes(b)]
        blend = now + beta * (now - before)
        nblend_ref[:, lanes(b)] = blend
        packed_ref[b] = blend.astype(jnp.bfloat16)
        xt[pl.ds(pl.multiple_of(b * TILE, TILE), TILE), :] = blend.T
        return carry

    lax.fori_loop(0, blocks, blend_block, 0, unroll=2)

    slot_range = lax.broadcasted_iota(jnp.int32, (1, slots), 1)
    GROUP = 16

    def gather_round(k):
        def group(g, carry):
            base = pl.multiple_of(g * GROUP, GROUP)
            for i in range(GROUP):
                gt[pl.ds(base + i, 1), :] = xt[pl.ds(idx_ref[k, base + i], 1), :]
            return carry

        lax.fori_loop(0, slots // GROUP, group, 0)
        moved = gt[...].T
        sbuf[k] = jnp.where(slot_range < cnt_ref[k], moved, 0.0).astype(jnp.bfloat16)

    def fixed(k):
        if k == 0:
            return parts - 1
        if k == 1:
            return parts // 2
        return 1 if k == rounds - 1 else None

    loose = [k for k in range(rounds) if fixed(k) is None]
    firm = [k for k in range(rounds) if fixed(k) is not None]

    def direct_copy(k):
        mask = fixed(k)
        return pltpu.make_async_remote_copy(
            src_ref=sbuf.at[k], dst_ref=direct.at[k], send_sem=d_send.at[k], recv_sem=d_recv.at[k],
            device_id=(flip(r, mask // cols), flip(c, mask % cols)), device_id_type=MESH)

    sends = []
    for n, k in enumerate(loose):
        gather_round(k)
        for j in range(1, cols):
            sends.append(pltpu.make_async_remote_copy(
                src_ref=sbuf.at[k], dst_ref=bcol.at[n, j], send_sem=c_send.at[n, j], recv_sem=c_recv.at[n, j],
                device_id=(r, flip(c, j)), device_id_type=MESH))
            sends[-1].start()
        bcol[n, 0] = sbuf[k]
    for k in firm:
        gather_round(k)
        copy = direct_copy(k)
        copy.start()
    col_sends = list(sends)
    row_sends = []
    for n, k in enumerate(loose):
        for copy in col_sends[n * (cols - 1):(n + 1) * (cols - 1)]:
            copy.wait_recv()
        picked[n] = bcol[n, masks_ref[k] % cols]
        for j in range(1, rows):
            copy = pltpu.make_async_remote_copy(
                src_ref=picked.at[n], dst_ref=brow.at[n, j], send_sem=r_send.at[n, j], recv_sem=r_recv.at[n, j],
                device_id=(flip(r, j), c), device_id_type=MESH)
            copy.start()
            row_sends.append(copy)
        brow[n, 0] = picked[n]
    for n, k in enumerate(loose):
        for copy in row_sends[n * (rows - 1):(n + 1) * (rows - 1)]:
            copy.wait_recv()
        recv_ref[k] = brow[n, masks_ref[k] // cols]
    for k in firm:
        direct_copy(k).wait_recv()
        recv_ref[k] = direct[k]
    for copy in col_sends + row_sends:
        copy.wait_send()
    for k in firm:
        direct_copy(k).wait_send()


def step(mode, rows, cols, nodes_all, cid, smalls, arrays):
    vm = pl.BlockSpec(memory_space=pltpu.VMEM)
    sm = pl.BlockSpec(memory_space=pltpu.SMEM)
    comps, nodes = arrays[0].shape
    f32, bf16 = jnp.float32, jnp.bfloat16
    dma = pltpu.SemaphoreType.DMA
    outs, scratch = [], []
    if mode != "first":
        outs.append(jax.ShapeDtypeStruct((comps, nodes), f32))
        scratch += [pltpu.VMEM((2, 8, TILE), f32), pltpu.VMEM((rows, 8, TILE), f32), pltpu.VMEM((cols, 8, TILE), f32)]
        scratch += [dma((rows + cols,)), dma((rows,)), dma((cols,))]
    if mode != "last":
        rounds, slots = smalls[0].shape
        loose = max(rounds - 3, 1)
        outs.append(jax.ShapeDtypeStruct((comps, nodes), f32))
        outs.append(jax.ShapeDtypeStruct((nodes // TILE, comps, TILE), bf16))
        outs.append(jax.ShapeDtypeStruct((rounds, comps, slots), bf16))
        scratch += [pltpu.VMEM((nodes, comps), f32), pltpu.VMEM((slots, comps), f32)]
        scratch += [pltpu.VMEM((rounds, comps, slots), bf16), pltpu.VMEM((rounds, comps, slots), bf16)]
        scratch += [pltpu.VMEM((loose, rows, comps, slots), bf16), pltpu.VMEM((loose, cols, comps, slots), bf16)]
        scratch += [pltpu.VMEM((loose, comps, slots), bf16)]
        scratch += [dma((rounds,)), dma((rounds,)), dma((loose, cols)), dma((loose, cols)), dma((loose, rows)), dma((loose, rows))]
    else:
        outs += [jax.ShapeDtypeStruct((1, TILE), f32)] * 2
    return pl.pallas_call(
        functools.partial(step_kernel, mode, rows, cols, nodes_all),
        out_shape=outs,
        in_specs=[sm] * len(smalls) + [vm] * len(arrays),
        out_specs=[vm] * len(outs),
        scratch_shapes=scratch,
        compiler_params=pltpu.CompilerParams(collective_id=cid, has_side_effects=True, vmem_limit_bytes=LIMIT),
        name="step_" + mode,
    )(*smalls, *arrays)


def apply_kernel(chunk, src_ref, dst_ref, tcnt_ref, idx_ref, cnt_ref, vals_ref, packed_ref, recv_ref, couple_ref, out_ref, acc, at, ext):
    pid = pl.program_id(0)
    blocks, comps, _ = packed_ref.shape
    rounds, slots = idx_ref.shape

    @pl.when(pid == 0)
    def _():
        acc[...] = jnp.zeros_like(acc)

    UN = 8

    def group(g, carry):
        prods = []
        for i in range(UN):
            t = g * UN + i
            prods.append(jnp.dot(packed_ref[src_ref[0, pid * chunk + t]], vals_ref[t], preferred_element_type=jnp.float32))
        for i in range(UN):
            t = pid * chunk + g * UN + i
            d = jnp.where(t < tcnt_ref[0], dst_ref[0, t], blocks)
            acc[d] += prods[i]
        return carry

    lax.fori_loop(0, chunk // UN, group, 0)

    @pl.when(pid == pl.num_programs(0) - 1)
    def _():
        at[...] = jnp.zeros_like(at)
        slot_range = lax.broadcasted_iota(jnp.int32, (1, slots), 1)
        for k in range(rounds):
            extra = jnp.dot(recv_ref[k], couple_ref[k], preferred_element_type=jnp.float32)
            ext[...] = jnp.where(slot_range < cnt_ref[k], extra, 0.0).T
            GROUP = 16

            def scatter(g, carry):
                base = pl.multiple_of(g * GROUP, GROUP)
                where = [idx_ref[k, base + i] for i in range(GROUP)]
                sums = [at[pl.ds(where[i], 1), :] + ext[pl.ds(base + i, 1), :] for i in range(GROUP)]
                for i in range(GROUP):
                    at[pl.ds(where[i], 1), :] = sums[i]
                return carry

            lax.fori_loop(0, slots // GROUP, scatter, 0)

        def finish(b, carry):
            span = pl.ds(pl.multiple_of(b * TILE, TILE), TILE)
            out_ref[:, span] = acc[b] + at[span, :].T
            return carry

        lax.fori_loop(0, blocks, finish, 0, unroll=2)


def apply_all(tile_src, tile_dst, tile_count, sep_idx, sep_count, tile_vals, packed, recv, couple):
    tiles = tile_vals.shape[0]
    chunk = 32 if tiles % 32 == 0 else 8
    blocks, comps, _ = packed.shape
    rounds, slots = sep_idx.shape
    nodes = blocks * TILE
    f32 = jnp.float32
    whole = lambda shape: pl.BlockSpec(shape, lambda i, *_: (0,) * len(shape))
    return pl.pallas_call(
        functools.partial(apply_kernel, chunk),
        out_shape=jax.ShapeDtypeStruct((comps, nodes), f32),
        grid_spec=pltpu.PrefetchScalarGridSpec(
            num_scalar_prefetch=5,
            grid=(tiles // chunk,),
            in_specs=[
                pl.BlockSpec((chunk, TILE, TILE), lambda i, *_: (i, 0, 0)),
                whole(packed.shape), whole(recv.shape), whole(couple.shape),
            ],
            out_specs=whole((comps, nodes)),
            scratch_shapes=[
                pltpu.VMEM((blocks + 1, comps, TILE), f32),
                pltpu.VMEM((nodes, comps), f32),
                pltpu.VMEM((slots, comps), f32),
            ],
        ),
        compiler_params=pltpu.CompilerParams(dimension_semantics=("arbitrary",), vmem_limit_bytes=LIMIT),
        name="apply_all",
    )(tile_src, tile_dst, tile_count, sep_idx, sep_count, tile_vals, packed, recv, couple)


def local(rows, cols, factor, prior, tile_src, tile_dst, tile_count, tile_vals, sep_idx, sep_count, couple, masks):
    nodes_all = rows * cols * factor.shape[1]
    smalls = (sep_idx[0], sep_count[0], masks)
    blend, packed, recv = step("first", rows, cols, nodes_all, 0, smalls, (factor, prior))
    current = factor
    for iterate in range(ITERS):
        applied = apply_all(tile_src, tile_dst, tile_count, sep_idx[0], sep_count[0], tile_vals, packed, recv, couple[0])
        if iterate < ITERS - 1:
            current, blend, packed, recv = step("middle", rows, cols, nodes_all, 1 + iterate, smalls, (current, blend, applied))
    current, beta, energy = step("last", rows, cols, nodes_all, ITERS, (), (current, blend, applied))
    return (current, beta[0, 0], energy[0, 0])


def solution(mesh):
    rows, cols = mesh.shape["row"], mesh.shape["col"]
    in_specs = (
        P(None, ("row", "col")),
        P(None, ("row", "col")),
        P(("row", "col"), None),
        P(("row", "col"), None),
        P(("row", "col")),
        P(("row", "col"), None, None),
        P(("row", "col"), None, None),
        P(("row", "col"), None),
        P(("row", "col"), None, None, None),
        P(),
    )
    out_specs = (P(None, ("row", "col")), P(), P())
    return jax.shard_map(functools.partial(local, rows, cols), mesh=mesh, in_specs=in_specs, out_specs=out_specs, check_vma=False)
```

```python
import functools

import jax
import jax.numpy as jnp
from jax import lax
from jax.experimental import pallas as pl
from jax.experimental.pallas import tpu as pltpu
from jax.sharding import PartitionSpec as P

TILE = 128
ITERS = 2
MOMENTUM_CAP = 0.9
MESH = pl.DeviceIdType.MESH
LIMIT = 60 * 1024 * 1024
UNROLL = 8
GROUP = 32


def flip(x, j):
    bit = 1
    while bit <= j:
        if j & bit:
            x = x + bit * (1 - 2 * ((x // bit) % 2))
        bit *= 2
    return x


def step_kernel(mode, rows, cols, nodes_all, *refs):
    first, last = mode == "first", mode == "last"
    parts = rows * cols
    refs = list(refs)
    take = lambda n: [refs.pop(0) for _ in range(n)]
    if not last:
        idx_ref, cnt_ref, masks_ref = take(3)
    if first:
        cur_ref, prior_ref = take(2)
    elif last:
        part_ref = take(1)[0]
    else:
        cur_ref, blend_ref, app_ref = take(3)
        new_ref = take(1)[0]
    if not last:
        nblend_ref, packed_ref, recv_ref = take(3)
    else:
        beta_ref, energy_ref = take(2)
    if not first:
        stat, srow, scol = take(3)
        st_send, st_rrow, st_rcol = take(3)
    if not last:
        xt, gt, sbuf, direct, brow, bcol, picked = take(7)
        d_send, d_recv, c_send, c_recv, r_send, r_recv = take(6)

    if not last:
        comps = cur_ref.shape[0]
        blocks = cur_ref.shape[1] // TILE
    r = lax.axis_index("row")
    c = lax.axis_index("col")

    barrier = pltpu.get_barrier_semaphore()
    peers = [(flip(r, j), c) for j in range(1, rows)] + [(r, flip(c, j)) for j in range(1, cols)]
    if not last:
        peers.append((flip(r, rows - 1), flip(c, cols - 1)))
    for peer in peers:
        pl.semaphore_signal(barrier, inc=1, device_id=peer, device_id_type=MESH)

    def lanes(b):
        return pl.ds(pl.multiple_of(b * TILE, TILE), TILE)

    if first:
        pl.semaphore_wait(barrier, len(peers))
        beta = 0.5 * MOMENTUM_CAP
    else:
        if not last:
            def norm_block(b, carry):
                change, total = carry
                applied = app_ref[:, lanes(b)]
                moved = blend_ref[:, lanes(b)] + applied
                length = jnp.sqrt(jnp.sum(moved * moved, axis=0, keepdims=True))
                updated = moved / jnp.maximum(length, 1.0)
                new_ref[:, lanes(b)] = updated
                return (change + applied * (updated - cur_ref[:, lanes(b)]), total + applied * updated)

            zero = jnp.zeros((comps, TILE), jnp.float32)
            change, total = lax.fori_loop(0, blocks, norm_block, (zero, zero), unroll=4)
            stat[...] = jnp.zeros_like(stat)
            stat[0, 0:1, :] = jnp.sum(change, axis=0, keepdims=True)
            stat[0, 1:2, :] = jnp.sum(total, axis=0, keepdims=True)
        else:
            stat[0] = part_ref[...]
        pl.semaphore_wait(barrier, len(peers))
        copies = []
        for j in range(1, rows):
            copies.append(pltpu.make_async_remote_copy(
                src_ref=stat.at[0], dst_ref=srow.at[r], send_sem=st_send.at[j],
                recv_sem=st_rrow.at[r], device_id=(flip(r, j), c), device_id_type=MESH))
        for copy in copies:
            copy.start()
        for j in range(1, rows):
            q = flip(r, j)
            pltpu.make_async_remote_copy(
                src_ref=stat.at[0], dst_ref=srow.at[q], send_sem=st_send.at[j],
                recv_sem=st_rrow.at[q], device_id=(q, c), device_id_type=MESH).wait_recv()
        mine = stat[0]
        both = jnp.where(r == 0, mine, srow[0])
        for q in range(1, rows):
            both = both + jnp.where(r == q, mine, srow[q])
        stat[1] = both
        more = []
        for j in range(1, cols):
            more.append(pltpu.make_async_remote_copy(
                src_ref=stat.at[1], dst_ref=scol.at[c], send_sem=st_send.at[rows + j],
                recv_sem=st_rcol.at[c], device_id=(r, flip(c, j)), device_id_type=MESH))
        for copy in more:
            copy.start()
        for j in range(1, cols):
            q = flip(c, j)
            pltpu.make_async_remote_copy(
                src_ref=stat.at[1], dst_ref=scol.at[q], send_sem=st_send.at[rows + j],
                recv_sem=st_rcol.at[q], device_id=(r, q), device_id_type=MESH).wait_recv()
        both = stat[1]
        every = jnp.where(c == 0, both, scol[0])
        for q in range(1, cols):
            every = every + jnp.where(c == q, both, scol[q])
        sums = jnp.sum(every, axis=1, keepdims=True) / nodes_all
        beta = MOMENTUM_CAP * 0.5 * (1.0 + jnp.tanh(sums[0:1]))
        if last:
            beta_ref[...] = jnp.broadcast_to(beta, beta_ref.shape)
            energy_ref[...] = jnp.broadcast_to(sums[1:2], energy_ref.shape)
        for copy in copies + more:
            copy.wait_send()

    if last:
        return

    rounds, slots = idx_ref.shape

    def blend_block(b, carry):
        if first:
            now, before = cur_ref[:, lanes(b)], prior_ref[:, lanes(b)]
        else:
            now, before = new_ref[:, lanes(b)], cur_ref[:, lanes(b)]
        blend = now + beta * (now - before)
        nblend_ref[:, lanes(b)] = blend
        packed_ref[b] = blend.astype(jnp.bfloat16)
        xt[pl.ds(pl.multiple_of(b * TILE, TILE), TILE), :] = blend.T
        return carry

    lax.fori_loop(0, blocks, blend_block, 0, unroll=4)

    slot_range = lax.broadcasted_iota(jnp.int32, (1, slots), 1)
    def gather_round(k):
        for j in range(slots):
            gt[j:j + 1, :] = xt[pl.ds(idx_ref[k, j], 1), :]
        moved = gt[...].T
        sbuf[k] = jnp.where(slot_range < cnt_ref[k], moved, 0.0).astype(jnp.bfloat16)

    def fixed(k):
        if k == 0:
            return parts - 1
        if k == 1:
            return parts // 2
        return 1 if k == rounds - 1 else None

    loose = [k for k in range(rounds) if fixed(k) is None]
    firm = [k for k in range(rounds) if fixed(k) is not None]

    def direct_copy(k):
        mask = fixed(k)
        return pltpu.make_async_remote_copy(
            src_ref=sbuf.at[k], dst_ref=direct.at[k], send_sem=d_send.at[k], recv_sem=d_recv.at[k],
            device_id=(flip(r, mask // cols), flip(c, mask % cols)), device_id_type=MESH)

    sends = []
    for n, k in enumerate(loose):
        gather_round(k)
        for j in range(1, cols):
            sends.append(pltpu.make_async_remote_copy(
                src_ref=sbuf.at[k], dst_ref=bcol.at[n, j], send_sem=c_send.at[n, j], recv_sem=c_recv.at[n, j],
                device_id=(r, flip(c, j)), device_id_type=MESH))
            sends[-1].start()
        bcol[n, 0] = sbuf[k]
    for k in firm:
        gather_round(k)
        copy = direct_copy(k)
        copy.start()
    col_sends = list(sends)
    row_sends = []
    for n, k in enumerate(loose):
        for copy in col_sends[n * (cols - 1):(n + 1) * (cols - 1)]:
            copy.wait_recv()
        picked[n] = bcol[n, masks_ref[k] % cols]
        for j in range(1, rows):
            copy = pltpu.make_async_remote_copy(
                src_ref=picked.at[n], dst_ref=brow.at[n, j], send_sem=r_send.at[n, j], recv_sem=r_recv.at[n, j],
                device_id=(flip(r, j), c), device_id_type=MESH)
            copy.start()
            row_sends.append(copy)
        brow[n, 0] = picked[n]
    for n, k in enumerate(loose):
        for copy in row_sends[n * (rows - 1):(n + 1) * (rows - 1)]:
            copy.wait_recv()
        recv_ref[k] = brow[n, masks_ref[k] // cols]
    for k in firm:
        direct_copy(k).wait_recv()
        recv_ref[k] = direct[k]
    for copy in col_sends + row_sends:
        copy.wait_send()
    for k in firm:
        direct_copy(k).wait_send()


def step(mode, rows, cols, nodes_all, cid, smalls, arrays):
    vm = pl.BlockSpec(memory_space=pltpu.VMEM)
    sm = pl.BlockSpec(memory_space=pltpu.SMEM)
    comps, nodes = arrays[0].shape
    f32, bf16 = jnp.float32, jnp.bfloat16
    dma = pltpu.SemaphoreType.DMA
    outs, scratch = [], []
    if mode != "first":
        if mode != "last":
            outs.append(jax.ShapeDtypeStruct((comps, nodes), f32))
        scratch += [pltpu.VMEM((2, 8, TILE), f32), pltpu.VMEM((rows, 8, TILE), f32), pltpu.VMEM((cols, 8, TILE), f32)]
        scratch += [dma((rows + cols,)), dma((rows,)), dma((cols,))]
    if mode != "last":
        rounds, slots = smalls[0].shape
        loose = max(rounds - 3, 1)
        outs.append(jax.ShapeDtypeStruct((comps, nodes), f32))
        outs.append(jax.ShapeDtypeStruct((nodes // TILE, comps, TILE), bf16))
        outs.append(jax.ShapeDtypeStruct((rounds, comps, slots), bf16))
        scratch += [pltpu.VMEM((nodes, comps), f32), pltpu.VMEM((slots, comps), f32)]
        scratch += [pltpu.VMEM((rounds, comps, slots), bf16), pltpu.VMEM((rounds, comps, slots), bf16)]
        scratch += [pltpu.VMEM((loose, rows, comps, slots), bf16), pltpu.VMEM((loose, cols, comps, slots), bf16)]
        scratch += [pltpu.VMEM((loose, comps, slots), bf16)]
        scratch += [dma((rounds,)), dma((rounds,)), dma((loose, cols)), dma((loose, cols)), dma((loose, rows)), dma((loose, rows))]
    else:
        outs += [jax.ShapeDtypeStruct((1, TILE), f32)] * 2
    return pl.pallas_call(
        functools.partial(step_kernel, mode, rows, cols, nodes_all),
        out_shape=outs,
        in_specs=[sm] * len(smalls) + [vm] * len(arrays),
        out_specs=[vm] * len(outs),
        scratch_shapes=scratch,
        compiler_params=pltpu.CompilerParams(collective_id=cid, has_side_effects=True, vmem_limit_bytes=LIMIT),
        name="step_" + mode,
    )(*smalls, *arrays)


def apply_kernel(chunk, last, src_ref, dst_ref, tcnt_ref, idx_ref, cnt_ref, vals_ref, packed_ref, recv_ref, couple_ref, *refs):
    if last:
        cur_ref, blend_ref, out_ref, stat_ref, acc, at, ext = refs
    else:
        out_ref, acc, at, ext = refs
    pid = pl.program_id(0)
    blocks, comps, _ = packed_ref.shape
    rounds, slots = idx_ref.shape

    @pl.when(pid == 0)
    def _():
        acc[...] = jnp.zeros_like(acc)

    for base in range(0, chunk, UNROLL):
        prods = []
        for t in range(base, base + UNROLL):
            prods.append(jnp.dot(packed_ref[src_ref[pid, t]], vals_ref[t], preferred_element_type=jnp.float32))
        for t in range(base, base + UNROLL):
            d = jnp.where(pid * chunk + t < tcnt_ref[0], dst_ref[pid, t], blocks)
            acc[d] += prods[t - base]

    @pl.when(pid == pl.num_programs(0) - 1)
    def _():
        at[...] = jnp.zeros_like(at)
        slot_range = lax.broadcasted_iota(jnp.int32, (1, slots), 1)
        for k in range(rounds):
            extra = jnp.dot(recv_ref[k], couple_ref[k], preferred_element_type=jnp.float32)
            ext[...] = jnp.where(slot_range < cnt_ref[k], extra, 0.0).T
            for base in range(0, slots, GROUP):
                where = [idx_ref[k, base + i] for i in range(GROUP)]
                sums = [at[pl.ds(where[i], 1), :] + ext[base + i:base + i + 1, :] for i in range(GROUP)]
                for i in range(GROUP):
                    at[pl.ds(where[i], 1), :] = sums[i]

        def applied_at(b):
            span = pl.ds(pl.multiple_of(b * TILE, TILE), TILE)
            return span, acc[b] + at[span, :].T

        if not last:
            def finish(b, carry):
                span, applied = applied_at(b)
                out_ref[:, span] = applied
                return carry

            lax.fori_loop(0, blocks, finish, 0, unroll=4)
        else:
            def finish(b, carry):
                change, total = carry
                span, applied = applied_at(b)
                moved = blend_ref[:, span] + applied
                length = jnp.sqrt(jnp.sum(moved * moved, axis=0, keepdims=True))
                updated = moved / jnp.maximum(length, 1.0)
                out_ref[:, span] = updated
                return (change + applied * (updated - cur_ref[:, span]), total + applied * updated)

            zero = jnp.zeros((comps, TILE), jnp.float32)
            change, total = lax.fori_loop(0, blocks, finish, (zero, zero), unroll=4)
            stat_ref[...] = jnp.zeros_like(stat_ref)
            stat_ref[0:1, :] = jnp.sum(change, axis=0, keepdims=True)
            stat_ref[1:2, :] = jnp.sum(total, axis=0, keepdims=True)


def apply_all(tile_src, tile_dst, tile_count, sep_idx, sep_count, tile_vals, packed, recv, couple, extras=()):
    tiles = tile_vals.shape[0]
    chunk = 32 if tiles % 32 == 0 else 8
    blocks, comps, _ = packed.shape
    rounds, slots = sep_idx.shape
    nodes = blocks * TILE
    outs = [(comps, nodes), (8, TILE)] if extras else [(comps, nodes)]
    f32 = jnp.float32
    whole = lambda shape: pl.BlockSpec(shape, lambda i, *_: (0,) * len(shape))
    return pl.pallas_call(
        functools.partial(apply_kernel, chunk, bool(extras)),
        out_shape=[jax.ShapeDtypeStruct(o, f32) for o in outs],
        grid_spec=pltpu.PrefetchScalarGridSpec(
            num_scalar_prefetch=5,
            grid=(tiles // chunk,),
            in_specs=[
                pl.BlockSpec((chunk, TILE, TILE), lambda i, *_: (i, 0, 0)),
                whole(packed.shape), whole(recv.shape), whole(couple.shape),
            ] + [whole(e.shape) for e in extras],
            out_specs=[whole(o) for o in outs],
            scratch_shapes=[
                pltpu.VMEM((blocks + 1, comps, TILE), f32),
                pltpu.VMEM((nodes, comps), f32),
                pltpu.VMEM((slots, comps), f32),
            ],
        ),
        compiler_params=pltpu.CompilerParams(dimension_semantics=("arbitrary",), vmem_limit_bytes=LIMIT),
        name="apply_all",
    )(tile_src.reshape(tiles // chunk, chunk), tile_dst.reshape(tiles // chunk, chunk), tile_count, sep_idx, sep_count, tile_vals, packed, recv, couple, *extras)


def local(rows, cols, factor, prior, tile_src, tile_dst, tile_count, tile_vals, sep_idx, sep_count, couple, masks):
    nodes_all = rows * cols * factor.shape[1]
    smalls = (sep_idx[0], sep_count[0], masks)
    blend, packed, recv = step("first", rows, cols, nodes_all, 0, smalls, (factor, prior))
    current = factor
    for iterate in range(ITERS):
        final = iterate == ITERS - 1
        result = apply_all(tile_src, tile_dst, tile_count, sep_idx[0], sep_count[0], tile_vals, packed, recv, couple[0], (current, blend) if final else ())
        if not final:
            current, blend, packed, recv = step("middle", rows, cols, nodes_all, 1 + iterate, smalls, (current, blend, *result))
    current, stat = result
    beta, energy = step("last", rows, cols, nodes_all, ITERS, (), (stat,))
    return (current, beta[0, 0], energy[0, 0])


def solution(mesh):
    rows, cols = mesh.shape["row"], mesh.shape["col"]
    in_specs = (
        P(None, ("row", "col")),
        P(None, ("row", "col")),
        P(("row", "col"), None),
        P(("row", "col"), None),
        P(("row", "col")),
        P(("row", "col"), None, None),
        P(("row", "col"), None, None),
        P(("row", "col"), None),
        P(("row", "col"), None, None, None),
        P(),
    )
    out_specs = (P(None, ("row", "col")), P(), P())
    return jax.shard_map(functools.partial(local, rows, cols), mesh=mesh, in_specs=in_specs, out_specs=out_specs, check_vma=False)
```

```python
import functools

import jax
import jax.numpy as jnp
from jax import lax
from jax.experimental import pallas as pl
from jax.experimental.pallas import tpu as pltpu
from jax.sharding import PartitionSpec as P

TILE = 128
ITERS = 2
MOMENTUM_CAP = 0.9
MESH = pl.DeviceIdType.MESH
LIMIT = 60 * 1024 * 1024
UNROLL = 8
BANKS = 1
SHIFT = 16
GROUP = 32


def flip(x, j):
    bit = 1
    while bit <= j:
        if j & bit:
            x = x + bit * (1 - 2 * ((x // bit) % 2))
        bit *= 2
    return x


def step_kernel(mode, rows, cols, nodes_all, *refs):
    first, last = mode == "first", mode == "last"
    parts = rows * cols
    refs = list(refs)
    take = lambda n: [refs.pop(0) for _ in range(n)]
    if not last:
        idx_ref, cnt_ref, masks_ref = take(3)
    if first:
        cur_ref, prior_ref = take(2)
    elif last:
        part_ref = take(1)[0]
    else:
        cur_ref, blend_ref, app_ref = take(3)
        new_ref = take(1)[0]
    if not last:
        nblend_ref, recv_ref = take(2)
    else:
        beta_ref, energy_ref = take(2)
    if not first:
        stat, srow, scol = take(3)
        st_send, st_rrow, st_rcol = take(3)
    if not last:
        xt, gt, sbuf, direct, brow, bcol, picked = take(7)
        d_send, d_recv, c_send, c_recv, r_send, r_recv = take(6)

    if not last:
        comps = cur_ref.shape[0]
        blocks = cur_ref.shape[1] // TILE
    r = lax.axis_index("row")
    c = lax.axis_index("col")

    barrier = pltpu.get_barrier_semaphore()
    peers = [(flip(r, j), c) for j in range(1, rows)] + [(r, flip(c, j)) for j in range(1, cols)]
    if not last:
        peers.append((flip(r, rows - 1), flip(c, cols - 1)))
    for peer in peers:
        pl.semaphore_signal(barrier, inc=1, device_id=peer, device_id_type=MESH)

    def lanes(b):
        return pl.ds(pl.multiple_of(b * TILE, TILE), TILE)

    if not last:
        _, rounds, slots = idx_ref.shape
        slot_range = lax.broadcasted_iota(jnp.int32, (1, slots), 1)

        def gather_round(k):
            for j in range(slots):
                gt[j:j + 1, :] = xt[pl.ds(idx_ref[0, k, j], 1), :]
            sbuf[k] = jnp.where(slot_range < cnt_ref[0, k], gt[...].T, 0.0).astype(jnp.bfloat16)

    def first_block(b, carry):
        blend = cur_ref[:, lanes(b)] + beta0 * (cur_ref[:, lanes(b)] - prior_ref[:, lanes(b)])
        nblend_ref[:, lanes(b)] = blend
        xt[lanes(b), :] = blend.T
        return carry

    def norm_block(b, carry):
        change, total = carry
        applied = app_ref[:, lanes(b)]
        moved = blend_ref[:, lanes(b)] + applied
        length = jnp.sqrt(jnp.sum(moved * moved, axis=0, keepdims=True))
        updated = moved / jnp.maximum(length, 1.0)
        delta = updated - cur_ref[:, lanes(b)]
        new_ref[:, lanes(b)] = updated
        xt[lanes(b), :] = jnp.concatenate([updated, delta], axis=0).T
        return (change + applied * delta, total + applied * updated)

    def stat_copy(stage, slot, q):
        src, dst = stat.at[stage], (srow, scol)[stage].at[slot]
        recv = (st_rrow, st_rcol)[stage].at[slot]
        where = (q, c) if stage == 0 else (r, q)
        return src, dst, recv, where

    def stat_send(stage):
        size, mine = ((rows, r), (cols, c))[stage]
        sent = []
        for j in range(1, size):
            src, dst, recv, where = stat_copy(stage, mine, flip(mine, j))
            sent.append(pltpu.make_async_remote_copy(
                src_ref=src, dst_ref=dst, send_sem=st_send.at[stage * rows + j], recv_sem=recv,
                device_id=where, device_id_type=MESH))
            sent[-1].start()
        return sent

    def stat_take(stage):
        size, mine = ((rows, r), (cols, c))[stage]
        for j in range(1, size):
            q = flip(mine, j)
            src, dst, recv, where = stat_copy(stage, q, q)
            pltpu.make_async_remote_copy(
                src_ref=src, dst_ref=dst, send_sem=st_send.at[stage * rows + j], recv_sem=recv,
                device_id=where, device_id_type=MESH).wait_recv()
        own = stat[stage]
        slots_in = (srow, scol)[stage]
        every = jnp.where(mine == 0, own, slots_in[0])
        for q in range(1, size):
            every = every + jnp.where(mine == q, own, slots_in[q])
        return every

    def stat_beta(every):
        sums = jnp.sum(every, axis=1, keepdims=True) / nodes_all
        return MOMENTUM_CAP * 0.5 * (1.0 + jnp.tanh(sums[0:1])), sums[1:2]

    beta0 = 0.5 * MOMENTUM_CAP
    stat_sends = []
    if first:
        lax.fori_loop(0, blocks, first_block, 0, unroll=4)
        pl.semaphore_wait(barrier, len(peers))
    else:
        stat[...] = jnp.zeros_like(stat)
        if last:
            stat[0] = part_ref[...]
        else:
            zero = jnp.zeros((comps, TILE), jnp.float32)
            change, total = lax.fori_loop(0, blocks, norm_block, (zero, zero), unroll=4)
            stat[0, 0:1, :] = jnp.sum(change, axis=0, keepdims=True)
            stat[0, 1:2, :] = jnp.sum(total, axis=0, keepdims=True)
        pl.semaphore_wait(barrier, len(peers))
        stat_sends += stat_send(0)
        if last:
            stat[1] = stat_take(0)
            stat_sends += stat_send(1)
            beta, energy = stat_beta(stat_take(1))
            beta_ref[...] = jnp.broadcast_to(beta, beta_ref.shape)
            energy_ref[...] = jnp.broadcast_to(energy, energy_ref.shape)
            for copy in stat_sends:
                copy.wait_send()
            return

    def fixed(k):
        if k == 0:
            return parts - 1
        if k == 1:
            return parts // 2
        return 1 if k == rounds - 1 else None

    loose = [k for k in range(rounds) if fixed(k) is None]
    firm = [k for k in range(rounds) if fixed(k) is not None]

    def direct_copy(k):
        mask = fixed(k)
        return pltpu.make_async_remote_copy(
            src_ref=sbuf.at[k], dst_ref=direct.at[k], send_sem=d_send.at[k], recv_sem=d_recv.at[k],
            device_id=(flip(r, mask // cols), flip(c, mask % cols)), device_id_type=MESH)

    sends = []
    for n, k in enumerate(loose):
        gather_round(k)
        for j in range(1, cols):
            sends.append(pltpu.make_async_remote_copy(
                src_ref=sbuf.at[k], dst_ref=bcol.at[n, j], send_sem=c_send.at[n, j], recv_sem=c_recv.at[n, j],
                device_id=(r, flip(c, j)), device_id_type=MESH))
            sends[-1].start()
        bcol[n, 0] = sbuf[k]
    if not first:
        stat[1] = stat_take(0)
        stat_sends += stat_send(1)
    for k in firm:
        gather_round(k)
        copy = direct_copy(k)
        copy.start()
    if not first:
        beta, _ = stat_beta(stat_take(1))

        def blend_block(b, carry):
            now = new_ref[:, lanes(b)]
            nblend_ref[:, lanes(b)] = now + beta * (now - cur_ref[:, lanes(b)])
            return carry

        lax.fori_loop(0, blocks, blend_block, 0, unroll=4)

    def taken(block):
        if first:
            return block
        whole = block.astype(jnp.float32)
        return (whole[:comps] + beta * whole[comps:]).astype(jnp.bfloat16)

    col_sends = list(sends)
    row_sends = []
    for n, k in enumerate(loose):
        for copy in col_sends[n * (cols - 1):(n + 1) * (cols - 1)]:
            copy.wait_recv()
        picked[n] = bcol[n, masks_ref[k] % cols]
        for j in range(1, rows):
            copy = pltpu.make_async_remote_copy(
                src_ref=picked.at[n], dst_ref=brow.at[n, j], send_sem=r_send.at[n, j], recv_sem=r_recv.at[n, j],
                device_id=(flip(r, j), c), device_id_type=MESH)
            copy.start()
            row_sends.append(copy)
        brow[n, 0] = picked[n]
    for n, k in enumerate(loose):
        for copy in row_sends[n * (rows - 1):(n + 1) * (rows - 1)]:
            copy.wait_recv()
        recv_ref[k] = taken(brow[n, masks_ref[k] // cols])
    for k in firm:
        direct_copy(k).wait_recv()
        recv_ref[k] = taken(direct[k])
    for copy in stat_sends + col_sends + row_sends:
        copy.wait_send()
    for k in firm:
        direct_copy(k).wait_send()


def step(mode, rows, cols, nodes_all, cid, smalls, arrays):
    vm = pl.BlockSpec(memory_space=pltpu.VMEM)
    sm = pl.BlockSpec(memory_space=pltpu.SMEM)
    comps, nodes = arrays[0].shape
    f32, bf16 = jnp.float32, jnp.bfloat16
    dma = pltpu.SemaphoreType.DMA
    outs, scratch = [], []
    if mode != "first":
        if mode != "last":
            outs.append(jax.ShapeDtypeStruct((comps, nodes), f32))
        scratch += [pltpu.VMEM((2, 8, TILE), f32), pltpu.VMEM((rows, 8, TILE), f32), pltpu.VMEM((cols, 8, TILE), f32)]
        scratch += [dma((rows + cols,)), dma((rows,)), dma((cols,))]
    if mode != "last":
        _, rounds, slots = smalls[0].shape
        loose = max(rounds - 3, 1)
        outs.append(jax.ShapeDtypeStruct((comps, nodes), f32))
        outs.append(jax.ShapeDtypeStruct((rounds, comps, slots), bf16))
        wide = comps if mode == "first" else 2 * comps
        scratch += [pltpu.VMEM((nodes, wide), f32), pltpu.VMEM((slots, wide), f32)]
        scratch += [pltpu.VMEM((rounds, wide, slots), bf16), pltpu.VMEM((rounds, wide, slots), bf16)]
        scratch += [pltpu.VMEM((loose, rows, wide, slots), bf16), pltpu.VMEM((loose, cols, wide, slots), bf16)]
        scratch += [pltpu.VMEM((loose, wide, slots), bf16)]
        scratch += [dma((rounds,)), dma((rounds,)), dma((loose, cols)), dma((loose, cols)), dma((loose, rows)), dma((loose, rows))]
    else:
        outs += [jax.ShapeDtypeStruct((1, TILE), f32)] * 2
    return pl.pallas_call(
        functools.partial(step_kernel, mode, rows, cols, nodes_all),
        out_shape=outs,
        in_specs=[sm] * len(smalls) + [vm] * len(arrays),
        out_specs=[vm] * len(outs),
        scratch_shapes=scratch,
        compiler_params=pltpu.CompilerParams(collective_id=cid, has_side_effects=True, vmem_limit_bytes=LIMIT),
        name="step_" + mode,
    )(*smalls, *arrays)


def apply_kernel(chunk, last, code_ref, idx_ref, cnt_ref, vals_ref, blend_ref, recv_ref, couple_ref, *refs):
    if last:
        cur_ref, out_ref, stat_ref, *acc, at, ext = refs
    else:
        out_ref, *acc, at, ext = refs
    pid = pl.program_id(0)
    comps, nodes = blend_ref.shape
    blocks = nodes // TILE
    _, rounds, slots = idx_ref.shape

    @pl.when(pid == 0)
    def _():
        for bank in acc:
            bank[...] = jnp.zeros_like(bank)

    for base in range(0, chunk, UNROLL):
        prods = []
        for t in range(base, base + UNROLL, 2):
            spots = [pl.ds(pl.multiple_of((code_ref[pid, t + i] & ((1 << SHIFT) - 1)) * TILE, TILE), TILE) for i in range(2)]
            pair = jnp.concatenate([blend_ref[:, spot] for spot in spots], axis=0).astype(jnp.bfloat16)
            side = jnp.concatenate([vals_ref[t], vals_ref[t + 1]], axis=1)
            both = jnp.dot(pair, side, preferred_element_type=jnp.float32)
            prods += [both[:comps, :TILE], both[comps:, TILE:]]
        for t in range(base, base + UNROLL):
            acc[t % BANKS][code_ref[pid, t] >> SHIFT] += prods[t - base]

    @pl.when(pid == pl.num_programs(0) - 1)
    def _():
        at[...] = jnp.zeros_like(at)
        slot_range = lax.broadcasted_iota(jnp.int32, (1, slots), 1)
        for k in range(rounds):
            extra = jnp.dot(recv_ref[k], couple_ref[k], preferred_element_type=jnp.float32)
            ext[...] = jnp.where(slot_range < cnt_ref[0, k], extra, 0.0).T
            for base in range(0, slots, GROUP):
                where = [idx_ref[0, k, base + i] for i in range(GROUP)]
                sums = [at[pl.ds(where[i], 1), :] + ext[base + i:base + i + 1, :] for i in range(GROUP)]
                for i in range(GROUP):
                    at[pl.ds(where[i], 1), :] = sums[i]

        def applied_at(b):
            span = pl.ds(pl.multiple_of(b * TILE, TILE), TILE)
            return span, sum(bank[b] for bank in acc) + at[span, :].T

        if not last:
            def finish(b, carry):
                span, applied = applied_at(b)
                out_ref[:, span] = applied
                return carry

            lax.fori_loop(0, blocks, finish, 0, unroll=4)
        else:
            def finish(b, carry):
                change, total = carry
                span, applied = applied_at(b)
                moved = blend_ref[:, span] + applied
                length = jnp.sqrt(jnp.sum(moved * moved, axis=0, keepdims=True))
                updated = moved / jnp.maximum(length, 1.0)
                out_ref[:, span] = updated
                return (change + applied * (updated - cur_ref[:, span]), total + applied * updated)

            zero = jnp.zeros((comps, TILE), jnp.float32)
            change, total = lax.fori_loop(0, blocks, finish, (zero, zero), unroll=4)
            stat_ref[...] = jnp.zeros_like(stat_ref)
            stat_ref[0:1, :] = jnp.sum(change, axis=0, keepdims=True)
            stat_ref[1:2, :] = jnp.sum(total, axis=0, keepdims=True)


def apply_all(code, sep_idx, sep_count, tile_vals, blend, recv, couple, extras=()):
    tiles = tile_vals.shape[0]
    chunk = code.shape[1]
    comps, nodes = blend.shape
    blocks = nodes // TILE
    _, rounds, slots = sep_idx.shape
    outs = [(comps, nodes), (8, TILE)] if extras else [(comps, nodes)]
    f32 = jnp.float32
    whole = lambda shape: pl.BlockSpec(shape, lambda i, *_: (0,) * len(shape))
    return pl.pallas_call(
        functools.partial(apply_kernel, chunk, bool(extras)),
        out_shape=[jax.ShapeDtypeStruct(o, f32) for o in outs],
        grid_spec=pltpu.PrefetchScalarGridSpec(
            num_scalar_prefetch=3,
            grid=(tiles // chunk,),
            in_specs=[
                pl.BlockSpec((chunk, TILE, TILE), lambda i, *_: (i, 0, 0)),
                whole(blend.shape), whole(recv.shape), whole(couple.shape),
            ] + [whole(e.shape) for e in extras],
            out_specs=[whole(o) for o in outs],
            scratch_shapes=[
                *[pltpu.VMEM((blocks + 1, comps, TILE), f32) for _ in range(BANKS)],
                pltpu.VMEM((nodes, comps), f32),
                pltpu.VMEM((slots, comps), f32),
            ],
        ),
        compiler_params=pltpu.CompilerParams(dimension_semantics=("arbitrary",), vmem_limit_bytes=LIMIT),
        name="apply_all",
    )(code, sep_idx, sep_count, tile_vals, blend, recv, couple, *extras)


def local(rows, cols, factor, prior, tile_src, tile_dst, tile_count, tile_vals, sep_idx, sep_count, couple, masks):
    nodes_all = rows * cols * factor.shape[1]
    smalls = (sep_idx, sep_count, masks)
    tiles, blocks = tile_src.shape[1], factor.shape[1] // TILE
    live = jnp.arange(tiles, dtype=jnp.int32)[None, :] < tile_count[0]
    chunk = 32 if tiles % 32 == 0 else 8
    code = (jnp.where(live, tile_dst, blocks) * (1 << SHIFT) + tile_src).reshape(tiles // chunk, chunk)
    blend, recv = step("first", rows, cols, nodes_all, 0, smalls, (factor, prior))
    current = factor
    for iterate in range(ITERS):
        final = iterate == ITERS - 1
        result = apply_all(code, sep_idx, sep_count, tile_vals, blend, recv, couple[0], (current,) if final else ())
        if not final:
            current, blend, recv = step("middle", rows, cols, nodes_all, 1 + iterate, smalls, (current, blend, *result))
    current, stat = result
    beta, energy = step("last", rows, cols, nodes_all, ITERS, (), (stat,))
    return (current, beta[0, 0], energy[0, 0])


def solution(mesh):
    rows, cols = mesh.shape["row"], mesh.shape["col"]
    in_specs = (
        P(None, ("row", "col")),
        P(None, ("row", "col")),
        P(("row", "col"), None),
        P(("row", "col"), None),
        P(("row", "col")),
        P(("row", "col"), None, None),
        P(("row", "col"), None, None),
        P(("row", "col"), None),
        P(("row", "col"), None, None, None),
        P(),
    )
    out_specs = (P(None, ("row", "col")), P(), P())
    return jax.shard_map(functools.partial(local, rows, cols), mesh=mesh, in_specs=in_specs, out_specs=out_specs, check_vma=False)
```
